32 devices in a mesh: scen: 8 (over y, x, core), bldg: 4 (over z).
Axes of the slice: x: 2, y: 2, z: 4, core: 2. Of those that a mesh axis runs over, the one named last changes fastest.
Arguments:
- demand: float32 [128, 1024, 96], P('scen', 'bldg'), may hold values from -6 to 6
- tariff: float32 [128, 96], P('scen'), may hold values from 0 to 0.5
- feeder_price: float32 [128, 8, 96], P('scen'), may hold values from 0 to 0.5
- multiplier: float32 [128, 1024, 96], P('scen', 'bldg'), may hold values from -2 to 2
- previous_mean: float32 [128, 1024, 96], P('scen', 'bldg'), may hold values from 0 to 1
- inverse: float32 [1024, 96, 96], P('bldg'), as said below
- power_limit: float32 [1024, 96], P('bldg'), may hold values from 0.5 to 2
- weights: float32 [128], P('scen'), may hold values from 0.1 to 1
- tree_node: int32 [2, 128], P(None, 'scen'), may hold values from 0 to 15, as said below
- building_feeder: int32 [1024], P('bldg'), may hold values from 0 to 7, as said below
- feeder_limit: float32 [8, 96], replicated, may hold values from 25.6 to 128
Outputs:
- plan: float32 [128, 1024, 96], P('scen', 'bldg')
- new_multiplier: float32 [128, 1024, 96], P('scen', 'bldg')
- new_price: float32 [128, 8, 96], P('scen')
The draws below stay inside these ranges and needn't reach their ends.
Inputs may be any that keep to these rules, and one draw needn't show every extreme that they name: `tree_node`: scenarios that share a third-section node share the second-section node; each third-section node holds 8 scenarios, each second-section node 16 scenarios. `building_feeder`: every feeder has exactly 128 buildings. `inverse`: symmetric with a positive diagonal.
All inputs are finite; a program needn't handle non-finite values.
Results may differ from the reference program's by a relative error of at most 0.0001.
Values sent between devices are 32-bit elements; how exact they have to be, the bound alone decides.
A program may use at most 128 MiB of HBM per device.

```python
import math
import jax
import jax.numpy as jnp
from jax import lax

SLOTS = 96
FEED = 128
PROX = 12
S = 128
B = 1024
F = 8
N2 = 16


def draw_inverse(key, part):
    first, second = jax.random.split(key)
    diagonal = jax.random.uniform(first, (B, SLOTS), jnp.float32, 0.3, 0.6)
    noise = 0.006 * jax.random.normal(second, (B, SLOTS, SLOTS), jnp.float32)
    symmetric = 0.5 * (noise + jnp.swapaxes(noise, 1, 2))
    eye_mask = jnp.eye(SLOTS, dtype=jnp.float32)[None, :, :]
    return (symmetric * (1.0 - eye_mask) + eye_mask * diagonal[:, :, None]).astype(jnp.float32)


def draw_tree_node(key, part):
    shuffled = jax.random.permutation(key, S)
    fine_node = shuffled % (S // 8)
    coarse_node = fine_node % 8
    return jnp.stack([coarse_node, fine_node]).astype(jnp.int32)


def draw_building_feeder(key, part):
    shuffled = jax.random.permutation(key, B)
    return (shuffled // FEED).astype(jnp.int32)


def steps_of(rng, dims, shards, least, high):
    gain, own = 1.0, jax.random.fold_in(rng, 6)
    for position, parts in shards:
        draws = jnp.exp(jax.random.uniform(jax.random.fold_in(own, position), (parts,), jnp.float32, least / len(shards), high / len(shards)))
        gain = gain * jnp.repeat(draws, dims[position] // parts).reshape([-1 if axis == position else 1 for axis in range(len(dims))])
    return gain


def normal_values(own_key, dims, deviation, most, shards=(), kind=jnp.bfloat16):
    values = jax.random.normal(own_key, dims, jnp.float32) * deviation
    if len(shards) > 0:
        values = steps_of(own_key, dims, shards, -0.22, 0.18) * values
    return jnp.clip(values, min=-most, max=most).astype(kind)


def setup_inputs(seed: int = 0) -> dict:
    key_of = jax.random.split(jax.random.key(seed), 12)
    demand = normal_values(key_of[0], (S, B, SLOTS), 1.0, 6.0, ((0, 8), (1, 4)), jnp.float32)
    tariff = jnp.clip(0.5 * jax.random.uniform(key_of[1], (S, SLOTS), jnp.float32) ** steps_of(key_of[1], (S, SLOTS), ((0, 8),), -0.2, 0.2), 0.0, 0.5)
    feeder_price = jnp.clip(0.5 * jax.random.uniform(key_of[2], (S, F, SLOTS), jnp.float32) ** steps_of(key_of[2], (S, F, SLOTS), ((0, 8),), -0.2, 0.2), 0.0, 0.5)
    multiplier = normal_values(key_of[3], (S, B, SLOTS), 0.3, 2.0, ((0, 8), (1, 4)), jnp.float32)
    previous_mean = jnp.clip(1.0 * jax.random.uniform(key_of[4], (S, B, SLOTS), jnp.float32) ** steps_of(key_of[4], (S, B, SLOTS), ((0, 8), (1, 4)), -0.2, 0.2), 0.0, 1.0)
    inverse = draw_inverse(jax.random.fold_in(key_of[11], 71), 0)
    power_limit = jnp.clip(0.5 + 1.5 * jax.random.uniform(key_of[6], (B, SLOTS), jnp.float32) ** steps_of(key_of[6], (B, SLOTS), ((0, 4),), -0.2, 0.2), 0.5, 2.0)
    weights = jnp.clip(jnp.exp(math.log(1.0) - 2.3025851 * jax.random.uniform(key_of[7], (S,), jnp.float32) ** steps_of(key_of[7], (S,), ((0, 8),), -0.2, 0.2)), 0.1, 1.0)
    tree_node = draw_tree_node(jax.random.fold_in(key_of[11], 71), 0)
    building_feeder = draw_building_feeder(jax.random.fold_in(key_of[11], 71), 0)
    feeder_limit = jnp.clip(jax.random.uniform(key_of[10], (F, SLOTS), jnp.float32, 25.6, 128.0), 25.6, 128.0)
    return dict(demand=demand, tariff=tariff, feeder_price=feeder_price, multiplier=multiplier, previous_mean=previous_mean, inverse=inverse, power_limit=power_limit, weights=weights, tree_node=tree_node, building_feeder=building_feeder, feeder_limit=feeder_limit)


HIGHEST = lax.Precision.HIGHEST


def solve_prox(demand, tariff, feeder_price, multiplier, previous_mean, inverse, power_limit, building_feeder, feeders):
    member = (building_feeder[:, None] == jnp.arange(feeders)[None, :]).astype(jnp.float32)
    local_price = jnp.einsum("bf,sft->sbt", member, feeder_price, precision=HIGHEST)
    linear = tariff[:, None, :] + local_price - demand
    fixed_part = 0.5 * previous_mean - linear - multiplier
    ceiling = power_limit[None, :, :]
    iterate = jnp.clip(previous_mean, 0.0, ceiling)
    scaled_dual = jnp.zeros_like(iterate)
    for iteration in range(PROX):
        right_side = iterate - scaled_dual + fixed_part
        primal = jnp.einsum("btk,sbk->sbt", inverse, right_side, precision=HIGHEST)
        updated = jnp.clip(primal + scaled_dual, 0.0, ceiling)
        scaled_dual = scaled_dual + primal - updated
        iterate = updated
    return iterate, member


def reference(demand, tariff, feeder_price, multiplier, previous_mean, inverse, power_limit, weights, tree_node, building_feeder, feeder_limit):
    plan, member = solve_prox(demand, tariff, feeder_price, multiplier, previous_mean, inverse, power_limit, building_feeder, F)
    section_len = SLOTS // 4
    tables = [jnp.ones((1, S), jnp.float32),
              (tree_node[0][None, :] == jnp.arange(8)[:, None]).astype(jnp.float32),
              (tree_node[1][None, :] == jnp.arange(N2)[:, None]).astype(jnp.float32)]
    pieces = []
    for level in range(3):
        weighted = tables[level] * weights[None, :]
        block = plan[:, :, level * section_len:(level + 1) * section_len]
        node_total = jnp.einsum("ns,sbt->nbt", weighted, block, precision=HIGHEST)
        node_weight = jnp.sum(weighted, axis=1)
        means = node_total / node_weight[:, None, None]
        pieces.append(jnp.einsum("ns,nbt->sbt", tables[level], means, precision=HIGHEST))
    pieces.append(plan[:, :, 3 * section_len:])
    mean = jnp.concatenate(pieces, axis=2)
    new_multiplier = multiplier + 0.5 * (plan - mean)
    load = jnp.einsum("bf,sbt->sft", member, plan, precision=HIGHEST)
    new_price = jnp.maximum(0.0, feeder_price + (load - feeder_limit[None, :, :]) / FEED)
    return plan, new_multiplier, new_price
```

```python
import jax
import jax.numpy as jnp
from jax import lax
from jax.experimental import pallas as pl
from jax.experimental.pallas import tpu as pltpu
from jax.sharding import PartitionSpec as P

FEED = 128
PROX = 12


HIGHEST = lax.Precision.HIGHEST


def node_tables(nodes, fine_count):
    root = jnp.ones((1, nodes.shape[1]), jnp.float32)
    coarse = (nodes[0][None, :] == jnp.arange(8)[:, None]).astype(jnp.float32)
    fine_table = (nodes[1][None, :] == jnp.arange(fine_count)[:, None]).astype(jnp.float32)
    return [root, coarse, fine_table]


def section_sums(tables, scen_weight, shared_part, section_len):
    sums_list = []
    totals_list = []
    for level in range(3):
        weighted = tables[level] * scen_weight[None, :]
        block = shared_part[:, :, level * section_len : (level + 1) * section_len]
        sums_list.append(jnp.einsum("ns,sbt->nbt", weighted, block, precision=HIGHEST))
        totals_list.append(jnp.sum(weighted, axis=1))
    return (sums_list, totals_list)


def spread_means(tables, sums_list, totals_list):
    pieces = []
    for level in range(3):
        means = sums_list[level] / totals_list[level][:, None, None]
        pieces.append(jnp.einsum("ns,nbt->sbt", tables[level], means, precision=HIGHEST))
    return jnp.concatenate(pieces, axis=2)


BLOCK = 16
LANES = 128


def prox_kernel(
    demand_ref, tariff_ref, price_ref, mult_ref, prev_ref, inv_ref, limit_ref, feeder_ref,
    plan_ref, load_ref, w_ref, fixed_ref, z_ref, u_ref, price_t_ref,
):
    step = pl.program_id(0)
    scen, block, slots = demand_ref.shape

    @pl.when(step == 0)
    def _():
        load_ref[...] = jnp.zeros_like(load_ref)
        price_t_ref[...] = tariff_ref[...][None] + jnp.transpose(price_ref[...], (1, 0, 2))

    prev = jnp.transpose(prev_ref[...], (1, 0, 2))
    rest = 0.5 * prev_ref[...] + demand_ref[...] - mult_ref[...]
    fixed_ref[...] = jnp.transpose(rest, (1, 0, 2))
    ceiling = limit_ref[...][:, None, :]
    z_ref[...] = jnp.clip(prev, 0.0, ceiling)
    u_ref[...] = jnp.zeros_like(u_ref)
    for b in range(block):
        fixed_ref[b] = fixed_ref[b] - price_t_ref[feeder_ref[step * block + b]]
        full = inv_ref[b]
        high = full.astype(jnp.bfloat16)
        w_ref[b, :, :slots] = high
        w_ref[b, :, LANES : LANES + slots] = (full - high.astype(jnp.float32)).astype(jnp.bfloat16)

    def iteration(i, carry):
        for b in range(block):
            z, u = z_ref[b], u_ref[b]
            right = z - u + fixed_ref[b]
            high = right.astype(jnp.bfloat16)
            low = (right - high.astype(jnp.float32)).astype(jnp.bfloat16)
            both = jnp.concatenate([high, low], axis=0)
            out = jnp.dot(both, w_ref[b], preferred_element_type=jnp.float32)
            primal = out[:scen, :slots] + (out[:scen, LANES : LANES + slots] + out[scen:, :slots])
            moved = primal + u
            fresh = jnp.clip(moved, 0.0, limit_ref[b : b + 1, :])
            z_ref[b] = fresh
            u_ref[b] = moved - fresh
        return carry

    lax.fori_loop(0, PROX, iteration, 0)
    for b in range(block):
        load_ref[feeder_ref[step * block + b]] += z_ref[b]
    plan_ref[...] = jnp.transpose(z_ref[...], (1, 0, 2))


def prox(demand, tariff, feeder_price, multiplier, previous_mean, inverse, power_limit, building_feeder):
    scen, count, slots = demand.shape
    feeders = feeder_price.shape[1]
    block = min(BLOCK, count)
    big = pl.BlockSpec((scen, block, slots), lambda i: (0, i, 0))
    whole2 = pl.BlockSpec((scen, slots), lambda i: (0, 0))
    whole3 = pl.BlockSpec((scen, feeders, slots), lambda i: (0, 0, 0))
    return pl.pallas_call(
        prox_kernel,
        grid=(count // block,),
        in_specs=[
            big, whole2, whole3, big, big,
            pl.BlockSpec((block, slots, slots), lambda i: (i, 0, 0)),
            pl.BlockSpec((block, slots), lambda i: (i, 0)),
            pl.BlockSpec(memory_space=pltpu.SMEM),
        ],
        out_specs=[big, pl.BlockSpec((feeders, scen, slots), lambda i: (0, 0, 0))],
        out_shape=[
            jax.ShapeDtypeStruct((scen, count, slots), jnp.float32),
            jax.ShapeDtypeStruct((feeders, scen, slots), jnp.float32),
        ],
        scratch_shapes=[
            pltpu.VMEM((block, slots, 2 * LANES), jnp.bfloat16),
            pltpu.VMEM((block, scen, slots), jnp.float32),
            pltpu.VMEM((block, scen, slots), jnp.float32),
            pltpu.VMEM((block, scen, slots), jnp.float32),
            pltpu.VMEM((feeders, scen, slots), jnp.float32),
        ],
        compiler_params=pltpu.CompilerParams(dimension_semantics=("arbitrary",), vmem_limit_bytes=40 * 2**20),
        name="prox",
    )(demand, tariff, feeder_price, multiplier, previous_mean, inverse, power_limit, building_feeder)


def per_device(
    demand,
    tariff,
    feeder_price,
    multiplier,
    previous_mean,
    inverse,
    power_limit,
    weights,
    tree_node,
    building_feeder,
    feeder_limit,
):
    slot_count = demand.shape[2]
    section_len = slot_count // 4
    iterate, partial_load = prox(
        demand, tariff, feeder_price, multiplier, previous_mean, inverse, power_limit, building_feeder
    )
    shared_part = iterate[:, :, : 3 * section_len]
    fine_count = lax.axis_size("scen") * demand.shape[0] // 8
    tables = node_tables(tree_node, fine_count)
    sums_list, totals_list = section_sums(tables, weights, shared_part, section_len)
    summed = lax.psum(
        (sums_list[0], sums_list[1], sums_list[2], totals_list[0], totals_list[1], totals_list[2]),
        "scen",
    )
    early_mean = spread_means(tables, list(summed[:3]), list(summed[3:]))
    mean = jnp.concatenate([early_mean, iterate[:, :, 3 * section_len :]], axis=2)
    new_multiplier = multiplier + 0.5 * (iterate - mean)
    feeder_load = jnp.transpose(lax.psum(partial_load, "bldg"), (1, 0, 2))
    new_price = jnp.maximum(0.0, feeder_price + (feeder_load - feeder_limit[None, :, :]) / FEED)
    return (iterate, new_multiplier, new_price)


def solution(mesh):
    in_specs = (
        P("scen", "bldg", None),
        P("scen", None),
        P("scen", None, None),
        P("scen", "bldg", None),
        P("scen", "bldg", None),
        P("bldg", None, None),
        P("bldg", None),
        P("scen"),
        P(None, "scen"),
        P("bldg"),
        P(),
    )
    out_specs = (P("scen", "bldg", None), P("scen", "bldg", None), P("scen", None, None))
    return jax.shard_map(
        per_device, mesh=mesh, in_specs=in_specs, out_specs=out_specs, check_vma=False
    )
```

```python
import functools

import jax
import jax.numpy as jnp
from jax import lax
from jax.experimental import pallas as pl
from jax.experimental.pallas import tpu as pltpu
from jax.sharding import PartitionSpec as P

FEED = 128
PROX = 12


BLOCK = 16
LANES = 128


def prox_kernel(
    demand_ref, tariff_ref, price_ref, mult_ref, prev_ref, inv_ref, limit_ref, feeder_ref,
    plan_ref, load_ref, w_ref, fixed_ref, z_ref, u_ref, price_t_ref,
):
    step = pl.program_id(0)
    scen, block, slots = demand_ref.shape

    @pl.when(step == 0)
    def _():
        load_ref[...] = jnp.zeros_like(load_ref)
        price_t_ref[...] = tariff_ref[...][None] + jnp.transpose(price_ref[...], (1, 0, 2))

    prev = jnp.transpose(prev_ref[...], (1, 0, 2))
    rest = 0.5 * prev_ref[...] + demand_ref[...] - mult_ref[...]
    fixed_ref[...] = jnp.transpose(rest, (1, 0, 2))
    ceiling = limit_ref[...][:, None, :]
    z_ref[...] = jnp.clip(prev, 0.0, ceiling)
    u_ref[...] = jnp.zeros_like(u_ref)
    for b in range(block):
        fixed_ref[b] = fixed_ref[b] - price_t_ref[feeder_ref[step * block + b]]
        full = inv_ref[b]
        high = full.astype(jnp.bfloat16)
        w_ref[b, :, :slots] = high
        w_ref[b, :, LANES : LANES + slots] = (full - high.astype(jnp.float32)).astype(jnp.bfloat16)

    def iteration(i, carry):
        for b in range(block):
            z, u = z_ref[b], u_ref[b]
            right = z - u + fixed_ref[b]
            high = right.astype(jnp.bfloat16)
            low = (right - high.astype(jnp.float32)).astype(jnp.bfloat16)
            both = jnp.concatenate([high, low], axis=0)
            out = jnp.dot(both, w_ref[b], preferred_element_type=jnp.float32)
            primal = out[:scen, :slots] + (out[:scen, LANES : LANES + slots] + out[scen:, :slots])
            moved = primal + u
            fresh = jnp.clip(moved, 0.0, limit_ref[b : b + 1, :])
            z_ref[b] = fresh
            u_ref[b] = moved - fresh
        return carry

    lax.fori_loop(0, PROX, iteration, 0)
    for b in range(block):
        load_ref[feeder_ref[step * block + b]] += z_ref[b]
    plan_ref[...] = jnp.transpose(z_ref[...], (1, 0, 2))


def prox(demand, tariff, feeder_price, multiplier, previous_mean, inverse, power_limit, building_feeder):
    scen, count, slots = demand.shape
    feeders = feeder_price.shape[1]
    block = min(BLOCK, count)
    big = pl.BlockSpec((scen, block, slots), lambda i: (0, i, 0))
    whole2 = pl.BlockSpec((scen, slots), lambda i: (0, 0))
    whole3 = pl.BlockSpec((scen, feeders, slots), lambda i: (0, 0, 0))
    return pl.pallas_call(
        prox_kernel,
        grid=(count // block,),
        in_specs=[
            big, whole2, whole3, big, big,
            pl.BlockSpec((block, slots, slots), lambda i: (i, 0, 0)),
            pl.BlockSpec((block, slots), lambda i: (i, 0)),
            pl.BlockSpec(memory_space=pltpu.SMEM),
        ],
        out_specs=[big, pl.BlockSpec((feeders, scen, slots), lambda i: (0, 0, 0))],
        out_shape=[
            jax.ShapeDtypeStruct((scen, count, slots), jnp.float32),
            jax.ShapeDtypeStruct((feeders, scen, slots), jnp.float32),
        ],
        scratch_shapes=[
            pltpu.VMEM((block, slots, 2 * LANES), jnp.bfloat16),
            pltpu.VMEM((block, scen, slots), jnp.float32),
            pltpu.VMEM((block, scen, slots), jnp.float32),
            pltpu.VMEM((block, scen, slots), jnp.float32),
            pltpu.VMEM((feeders, scen, slots), jnp.float32),
        ],
        compiler_params=pltpu.CompilerParams(dimension_semantics=("arbitrary",), vmem_limit_bytes=40 * 2**20),
        name="prox",
    )(demand, tariff, feeder_price, multiplier, previous_mean, inverse, power_limit, building_feeder)


COARSE = 8


def sums_kernel(weighted_ref, plan_ref, out_ref):
    nodes, scen = weighted_ref.shape
    lanes = plan_ref.shape[2]
    length = plan_ref.shape[1] // 4
    tail = nodes * length
    out_ref[pl.ds(tail, out_ref.shape[0] - tail), :] = jnp.zeros((out_ref.shape[0] - tail, lanes), jnp.float32)

    def add_node(level):
        def body(n, carry):
            factor = weighted_ref[n, 0]
            total = factor
            acc = factor * plan_ref[0, level * length : (level + 1) * length, :]
            for s in range(1, scen):
                factor = weighted_ref[n, s]
                total = total + factor
                acc = acc + factor * plan_ref[s, level * length : (level + 1) * length, :]
            out_ref[pl.ds(pl.multiple_of(n * length, 8), length), :] = acc
            out_ref[pl.ds(tail + n, 1), :] = jnp.full((1, lanes), total, jnp.float32)
            return carry

        return body

    for level, (low, high) in enumerate(((0, 1), (1, 1 + COARSE), (1 + COARSE, nodes))):
        lax.fori_loop(low, high, add_node(level), 0)


def node_sums(weighted, plan_t, length, devices):
    nodes = weighted.shape[0]
    unit = 8 * devices
    rows = (nodes * length + nodes + unit - 1) // unit * unit
    return pl.pallas_call(
        sums_kernel,
        in_specs=[pl.BlockSpec(memory_space=pltpu.SMEM), pl.BlockSpec(memory_space=pltpu.VMEM)],
        out_specs=pl.BlockSpec(memory_space=pltpu.VMEM),
        out_shape=jax.ShapeDtypeStruct((rows, plan_t.shape[2]), jnp.float32),
        compiler_params=pltpu.CompilerParams(vmem_limit_bytes=24 * 2**20),
        name="node_sums",
    )(weighted, plan_t)


def exchange_kernel(
    scen_size, bldg_size, sums_ref, load_ref, full_ref, total_ref,
    landed, own, load_landed, all_rows, rs_send, rs_recv, ag_send, ag_recv, load_send, load_recv,
):
    me, column = lax.axis_index("scen"), lax.axis_index("bldg")
    chunk = own.shape[0]
    peers = [(lax.rem(me + k, scen_size), column) for k in range(1, scen_size)]
    beside = [(me, lax.rem(column + k, bldg_size)) for k in range(1, bldg_size)]
    barrier = pltpu.get_barrier_semaphore()
    for peer in peers + beside:
        pl.semaphore_signal(barrier, inc=1, device_id=peer, device_id_type=pl.DeviceIdType.MESH)
    pl.semaphore_wait(barrier, scen_size + bldg_size - 2)

    def rows_of(index):
        return pl.ds(pl.multiple_of(index * chunk, 8), chunk)

    scatter = []
    for k, peer in enumerate(peers):
        copy = pltpu.make_async_remote_copy(
            src_ref=sums_ref.at[rows_of(peer[0])], dst_ref=landed.at[k],
            send_sem=rs_send.at[k], recv_sem=rs_recv.at[k],
            device_id=peer, device_id_type=pl.DeviceIdType.MESH,
        )
        copy.start()
        scatter.append(copy)
    loads = []
    for k, peer in enumerate(beside):
        copy = pltpu.make_async_remote_copy(
            src_ref=load_ref, dst_ref=load_landed.at[k],
            send_sem=load_send.at[k], recv_sem=load_recv.at[k],
            device_id=peer, device_id_type=pl.DeviceIdType.MESH,
        )
        copy.start()
        loads.append(copy)
    for copy in scatter:
        copy.wait_recv()
    acc = sums_ref[rows_of(me), :]
    for k in range(scen_size - 1):
        acc = acc + landed[k]
    own[...] = acc
    all_rows[rows_of(me), :] = acc
    gather = []
    for k, peer in enumerate(peers):
        copy = pltpu.make_async_remote_copy(
            src_ref=own, dst_ref=all_rows.at[rows_of(me)],
            send_sem=ag_send.at[k], recv_sem=ag_recv.at[k],
            device_id=peer, device_id_type=pl.DeviceIdType.MESH,
        )
        copy.start()
        gather.append(copy)
    for copy in loads:
        copy.wait_recv()
    total = load_ref[...]
    for k in range(bldg_size - 1):
        total = total + load_landed[k]
    total_ref[...] = total
    for copy in gather:
        copy.wait_recv()
    full_ref[...] = all_rows[...]
    for copy in scatter + loads + gather:
        copy.wait_send()


def exchange(local, load):
    scen_size, bldg_size = lax.axis_size("scen"), lax.axis_size("bldg")
    rows, lanes = local.shape
    chunk = rows // scen_size
    dma = pltpu.SemaphoreType.DMA
    vmem = pl.BlockSpec(memory_space=pltpu.VMEM)
    return pl.pallas_call(
        functools.partial(exchange_kernel, scen_size, bldg_size),
        in_specs=[vmem, vmem],
        out_specs=[vmem, vmem],
        out_shape=[
            jax.ShapeDtypeStruct((rows, lanes), jnp.float32),
            jax.ShapeDtypeStruct(load.shape, jnp.float32),
        ],
        scratch_shapes=[
            pltpu.VMEM((scen_size - 1, chunk, lanes), jnp.float32),
            pltpu.VMEM((chunk, lanes), jnp.float32),
            pltpu.VMEM((bldg_size - 1,) + load.shape, jnp.float32),
            pltpu.VMEM((rows, lanes), jnp.float32),
            dma((scen_size - 1,)), dma((scen_size - 1,)),
            dma((scen_size - 1,)), dma((scen_size - 1,)),
            dma((bldg_size - 1,)), dma((bldg_size - 1,)),
        ],
        compiler_params=pltpu.CompilerParams(
            collective_id=0, has_side_effects=True, vmem_limit_bytes=24 * 2**20
        ),
        name="exchange",
    )(local, load)


def spread_kernel(nodes, places_ref, full_ref, plan_ref, mult_ref, out_ref, mean_ref):
    scen, slots, _ = plan_ref.shape
    length = slots // 4
    tail = nodes * length

    def divide(n, carry):
        share = full_ref[pl.ds(pl.multiple_of(n * length, 8), length), :]
        mean_ref[n] = share / full_ref[pl.ds(tail + n, 1), :]
        return carry

    lax.fori_loop(0, nodes, divide, 0)
    for s in range(scen):
        for level in range(4):
            part = slice(level * length, (level + 1) * length)
            plan = plan_ref[s, part, :]
            mean = plan if level == 3 else mean_ref[places_ref[level, s]]
            out_ref[s, part, :] = mult_ref[s, part, :] + 0.5 * (plan - mean)


def spread(places, full, plan_t, mult_t, nodes):
    vmem = pl.BlockSpec(memory_space=pltpu.VMEM)
    return pl.pallas_call(
        functools.partial(spread_kernel, nodes),
        in_specs=[pl.BlockSpec(memory_space=pltpu.SMEM), vmem, vmem, vmem],
        out_specs=vmem,
        out_shape=jax.ShapeDtypeStruct(plan_t.shape, jnp.float32),
        scratch_shapes=[pltpu.VMEM((nodes, plan_t.shape[1] // 4, plan_t.shape[2]), jnp.float32)],
        compiler_params=pltpu.CompilerParams(vmem_limit_bytes=24 * 2**20),
        name="spread",
    )(places, full, plan_t, mult_t)


def per_device(
    demand,
    tariff,
    feeder_price,
    multiplier,
    previous_mean,
    inverse,
    power_limit,
    weights,
    tree_node,
    building_feeder,
    feeder_limit,
):
    slot_count = demand.shape[2]
    section_len = slot_count // 4
    iterate, partial_load = prox(
        demand, tariff, feeder_price, multiplier, previous_mean, inverse, power_limit, building_feeder
    )
    plan_t = jnp.transpose(iterate, (0, 2, 1))
    mult_t = jnp.transpose(multiplier, (0, 2, 1))
    devices = lax.axis_size("scen")
    fine_count = devices * demand.shape[0] // 8
    offsets = jnp.array([[1], [1 + COARSE]], jnp.int32)
    places = jnp.concatenate([jnp.zeros_like(tree_node[:1]), tree_node + offsets], axis=0)
    nodes = 1 + COARSE + fine_count
    hits = places[:, None, :] == jnp.arange(nodes)[None, :, None]
    weighted = jnp.sum(hits.astype(jnp.float32), axis=0) * weights[None, :]
    local = node_sums(weighted, plan_t, section_len, devices)
    full, feeder_load = exchange(local, partial_load)
    new_multiplier = jnp.transpose(spread(places, full, plan_t, mult_t, nodes), (0, 2, 1))
    feeder_load = jnp.transpose(feeder_load, (1, 0, 2))
    new_price = jnp.maximum(0.0, feeder_price + (feeder_load - feeder_limit[None, :, :]) / FEED)
    return (iterate, new_multiplier, new_price)


def solution(mesh):
    in_specs = (
        P("scen", "bldg", None),
        P("scen", None),
        P("scen", None, None),
        P("scen", "bldg", None),
        P("scen", "bldg", None),
        P("bldg", None, None),
        P("bldg", None),
        P("scen"),
        P(None, "scen"),
        P("bldg"),
        P(),
    )
    out_specs = (P("scen", "bldg", None), P("scen", "bldg", None), P("scen", None, None))
    return jax.shard_map(
        per_device, mesh=mesh, in_specs=in_specs, out_specs=out_specs, check_vma=False
    )
```

```python
import functools

import jax
import jax.numpy as jnp
from jax import lax
from jax.experimental import pallas as pl
from jax.experimental.pallas import tpu as pltpu
from jax.sharding import PartitionSpec as P

FEED = 128
PROX = 12


BLOCK = 64
LANES = 128


def prox_kernel(
    demand_ref, tariff_ref, price_ref, mult_ref, prev_ref, inv_ref, limit_ref, feeder_ref,
    plan_ref, load_ref, w_ref, fixed_ref, z_ref, u_ref, price_t_ref,
):
    step = pl.program_id(0)
    scen, block, slots = demand_ref.shape

    @pl.when(step == 0)
    def _():
        load_ref[...] = jnp.zeros_like(load_ref)
        price_t_ref[...] = tariff_ref[...][None] + jnp.transpose(price_ref[...], (1, 0, 2))

    prev = jnp.transpose(prev_ref[...], (1, 0, 2))
    rest = 0.5 * prev_ref[...] + demand_ref[...] - mult_ref[...]
    fixed_ref[...] = jnp.transpose(rest, (1, 0, 2))
    ceiling = limit_ref[...][:, None, :]
    z_ref[...] = jnp.clip(prev, 0.0, ceiling)
    u_ref[...] = jnp.zeros_like(u_ref)
    for b in range(block):
        fixed_ref[b] = fixed_ref[b] - price_t_ref[feeder_ref[step * block + b]]
        full = inv_ref[b]
        high = full.astype(jnp.bfloat16)
        w_ref[b, :, :slots] = high
        w_ref[b, :, LANES : LANES + slots] = (full - high.astype(jnp.float32)).astype(jnp.bfloat16)

    def iteration(i, carry):
        for b in range(block):
            z, u = z_ref[b], u_ref[b]
            right = z - u + fixed_ref[b]
            high = right.astype(jnp.bfloat16)
            low = (right - high.astype(jnp.float32)).astype(jnp.bfloat16)
            both = jnp.concatenate([high, low], axis=0)
            out = jnp.dot(both, w_ref[b], preferred_element_type=jnp.float32)
            primal = out[:scen, :slots] + (out[:scen, LANES : LANES + slots] + out[scen:, :slots])
            moved = primal + u
            fresh = jnp.clip(moved, 0.0, limit_ref[b : b + 1, :])
            z_ref[b] = fresh
            u_ref[b] = moved - fresh
        return carry

    lax.fori_loop(0, PROX, iteration, 0)
    for b in range(block):
        load_ref[feeder_ref[step * block + b]] += z_ref[b]
    plan_ref[...] = jnp.transpose(z_ref[...], (1, 0, 2))


def prox(demand, tariff, feeder_price, multiplier, previous_mean, inverse, power_limit, building_feeder):
    scen, count, slots = demand.shape
    feeders = feeder_price.shape[1]
    block = min(BLOCK, count)
    big = pl.BlockSpec((scen, block, slots), lambda i: (0, i, 0))
    whole2 = pl.BlockSpec((scen, slots), lambda i: (0, 0))
    whole3 = pl.BlockSpec((scen, feeders, slots), lambda i: (0, 0, 0))
    return pl.pallas_call(
        prox_kernel,
        grid=(count // block,),
        in_specs=[
            big, whole2, whole3, big, big,
            pl.BlockSpec((block, slots, slots), lambda i: (i, 0, 0)),
            pl.BlockSpec((block, slots), lambda i: (i, 0)),
            pl.BlockSpec(memory_space=pltpu.SMEM),
        ],
        out_specs=[big, pl.BlockSpec((feeders, scen, slots), lambda i: (0, 0, 0))],
        out_shape=[
            jax.ShapeDtypeStruct((scen, count, slots), jnp.float32),
            jax.ShapeDtypeStruct((feeders, scen, slots), jnp.float32),
        ],
        scratch_shapes=[
            pltpu.VMEM((block, slots, 2 * LANES), jnp.bfloat16),
            pltpu.VMEM((block, scen, slots), jnp.float32),
            pltpu.VMEM((block, scen, slots), jnp.float32),
            pltpu.VMEM((block, scen, slots), jnp.float32),
            pltpu.VMEM((feeders, scen, slots), jnp.float32),
        ],
        compiler_params=pltpu.CompilerParams(dimension_semantics=("arbitrary",), vmem_limit_bytes=40 * 2**20),
        name="prox",
    )(demand, tariff, feeder_price, multiplier, previous_mean, inverse, power_limit, building_feeder)


COARSE = 8


def sums_kernel(weighted_ref, plan_ref, out_ref):
    nodes, scen = weighted_ref.shape
    lanes = plan_ref.shape[2]
    length = plan_ref.shape[1] // 4
    tail = nodes * length
    out_ref[pl.ds(tail, out_ref.shape[0] - tail), :] = jnp.zeros((out_ref.shape[0] - tail, lanes), jnp.float32)

    def add_node(level):
        def body(n, carry):
            factor = weighted_ref[n, 0]
            total = factor
            acc = factor * plan_ref[0, level * length : (level + 1) * length, :]
            for s in range(1, scen):
                factor = weighted_ref[n, s]
                total = total + factor
                acc = acc + factor * plan_ref[s, level * length : (level + 1) * length, :]
            out_ref[pl.ds(pl.multiple_of(n * length, 8), length), :] = acc
            out_ref[pl.ds(tail + n, 1), :] = jnp.full((1, lanes), total, jnp.float32)
            return carry

        return body

    for level, (low, high) in enumerate(((0, 1), (1, 1 + COARSE), (1 + COARSE, nodes))):
        lax.fori_loop(low, high, add_node(level), 0)


def node_sums(weighted, plan_t, length, devices):
    nodes = weighted.shape[0]
    unit = 8 * devices
    rows = (nodes * length + nodes + unit - 1) // unit * unit
    return pl.pallas_call(
        sums_kernel,
        in_specs=[pl.BlockSpec(memory_space=pltpu.SMEM), pl.BlockSpec(memory_space=pltpu.VMEM)],
        out_specs=pl.BlockSpec(memory_space=pltpu.VMEM),
        out_shape=jax.ShapeDtypeStruct((rows, plan_t.shape[2]), jnp.float32),
        compiler_params=pltpu.CompilerParams(vmem_limit_bytes=24 * 2**20),
        name="node_sums",
    )(weighted, plan_t)


def exchange_kernel(
    scen_size, bldg_size, sums_ref, load_ref, full_ref, total_ref,
    landed, own, load_landed, all_rows, rs_send, rs_recv, ag_send, ag_recv, load_send, load_recv,
):
    me, column = lax.axis_index("scen"), lax.axis_index("bldg")
    chunk = own.shape[0]
    peers = [(lax.rem(me + k, scen_size), column) for k in range(1, scen_size)]
    beside = [(me, lax.rem(column + k, bldg_size)) for k in range(1, bldg_size)]
    barrier = pltpu.get_barrier_semaphore()
    for peer in peers + beside:
        pl.semaphore_signal(barrier, inc=1, device_id=peer, device_id_type=pl.DeviceIdType.MESH)
    pl.semaphore_wait(barrier, scen_size + bldg_size - 2)

    def rows_of(index):
        return pl.ds(pl.multiple_of(index * chunk, 8), chunk)

    scatter = []
    for k, peer in enumerate(peers):
        copy = pltpu.make_async_remote_copy(
            src_ref=sums_ref.at[rows_of(peer[0])], dst_ref=landed.at[k],
            send_sem=rs_send.at[k], recv_sem=rs_recv.at[k],
            device_id=peer, device_id_type=pl.DeviceIdType.MESH,
        )
        copy.start()
        scatter.append(copy)
    loads = []
    for k, peer in enumerate(beside):
        copy = pltpu.make_async_remote_copy(
            src_ref=load_ref, dst_ref=load_landed.at[k],
            send_sem=load_send.at[k], recv_sem=load_recv.at[k],
            device_id=peer, device_id_type=pl.DeviceIdType.MESH,
        )
        copy.start()
        loads.append(copy)
    for copy in scatter:
        copy.wait_recv()
    acc = sums_ref[rows_of(me), :]
    for k in range(scen_size - 1):
        acc = acc + landed[k]
    own[...] = acc
    all_rows[rows_of(me), :] = acc
    gather = []
    for k, peer in enumerate(peers):
        copy = pltpu.make_async_remote_copy(
            src_ref=own, dst_ref=all_rows.at[rows_of(me)],
            send_sem=ag_send.at[k], recv_sem=ag_recv.at[k],
            device_id=peer, device_id_type=pl.DeviceIdType.MESH,
        )
        copy.start()
        gather.append(copy)
    for copy in loads:
        copy.wait_recv()
    total = load_ref[...]
    for k in range(bldg_size - 1):
        total = total + load_landed[k]
    total_ref[...] = total
    for copy in gather:
        copy.wait_recv()
    full_ref[...] = all_rows[...]
    for copy in scatter + loads + gather:
        copy.wait_send()


def exchange(local, load):
    scen_size, bldg_size = lax.axis_size("scen"), lax.axis_size("bldg")
    rows, lanes = local.shape
    chunk = rows // scen_size
    dma = pltpu.SemaphoreType.DMA
    vmem = pl.BlockSpec(memory_space=pltpu.VMEM)
    return pl.pallas_call(
        functools.partial(exchange_kernel, scen_size, bldg_size),
        in_specs=[vmem, vmem],
        out_specs=[vmem, vmem],
        out_shape=[
            jax.ShapeDtypeStruct((rows, lanes), jnp.float32),
            jax.ShapeDtypeStruct(load.shape, jnp.float32),
        ],
        scratch_shapes=[
            pltpu.VMEM((scen_size - 1, chunk, lanes), jnp.float32),
            pltpu.VMEM((chunk, lanes), jnp.float32),
            pltpu.VMEM((bldg_size - 1,) + load.shape, jnp.float32),
            pltpu.VMEM((rows, lanes), jnp.float32),
            dma((scen_size - 1,)), dma((scen_size - 1,)),
            dma((scen_size - 1,)), dma((scen_size - 1,)),
            dma((bldg_size - 1,)), dma((bldg_size - 1,)),
        ],
        compiler_params=pltpu.CompilerParams(
            collective_id=0, has_side_effects=True, vmem_limit_bytes=24 * 2**20
        ),
        name="exchange",
    )(local, load)


def spread_kernel(nodes, places_ref, full_ref, plan_ref, mult_ref, out_ref, mean_ref):
    scen, slots, _ = plan_ref.shape
    length = slots // 4
    tail = nodes * length

    def divide(n, carry):
        share = full_ref[pl.ds(pl.multiple_of(n * length, 8), length), :]
        mean_ref[n] = share / full_ref[pl.ds(tail + n, 1), :]
        return carry

    lax.fori_loop(0, nodes, divide, 0)
    for s in range(scen):
        for level in range(4):
            part = slice(level * length, (level + 1) * length)
            plan = plan_ref[s, part, :]
            mean = plan if level == 3 else mean_ref[places_ref[level, s]]
            out_ref[s, part, :] = mult_ref[s, part, :] + 0.5 * (plan - mean)


def spread(places, full, plan_t, mult_t, nodes):
    vmem = pl.BlockSpec(memory_space=pltpu.VMEM)
    return pl.pallas_call(
        functools.partial(spread_kernel, nodes),
        in_specs=[pl.BlockSpec(memory_space=pltpu.SMEM), vmem, vmem, vmem],
        out_specs=vmem,
        out_shape=jax.ShapeDtypeStruct(plan_t.shape, jnp.float32),
        scratch_shapes=[pltpu.VMEM((nodes, plan_t.shape[1] // 4, plan_t.shape[2]), jnp.float32)],
        compiler_params=pltpu.CompilerParams(vmem_limit_bytes=24 * 2**20),
        name="spread",
    )(places, full, plan_t, mult_t)


def per_device(
    demand,
    tariff,
    feeder_price,
    multiplier,
    previous_mean,
    inverse,
    power_limit,
    weights,
    tree_node,
    building_feeder,
    feeder_limit,
):
    slot_count = demand.shape[2]
    section_len = slot_count // 4
    iterate, partial_load = prox(
        demand, tariff, feeder_price, multiplier, previous_mean, inverse, power_limit, building_feeder
    )
    plan_t = jnp.transpose(iterate, (0, 2, 1))
    mult_t = jnp.transpose(multiplier, (0, 2, 1))
    devices = lax.axis_size("scen")
    fine_count = devices * demand.shape[0] // 8
    offsets = jnp.array([[1], [1 + COARSE]], jnp.int32)
    places = jnp.concatenate([jnp.zeros_like(tree_node[:1]), tree_node + offsets], axis=0)
    nodes = 1 + COARSE + fine_count
    hits = places[:, None, :] == jnp.arange(nodes)[None, :, None]
    weighted = jnp.sum(hits.astype(jnp.float32), axis=0) * weights[None, :]
    local = node_sums(weighted, plan_t, section_len, devices)
    full, feeder_load = exchange(local, partial_load)
    new_multiplier = jnp.transpose(spread(places, full, plan_t, mult_t, nodes), (0, 2, 1))
    feeder_load = jnp.transpose(feeder_load, (1, 0, 2))
    new_price = jnp.maximum(0.0, feeder_price + (feeder_load - feeder_limit[None, :, :]) / FEED)
    return (iterate, new_multiplier, new_price)


def solution(mesh):
    in_specs = (
        P("scen", "bldg", None),
        P("scen", None),
        P("scen", None, None),
        P("scen", "bldg", None),
        P("scen", "bldg", None),
        P("bldg", None, None),
        P("bldg", None),
        P("scen"),
        P(None, "scen"),
        P("bldg"),
        P(),
    )
    out_specs = (P("scen", "bldg", None), P("scen", "bldg", None), P("scen", None, None))
    return jax.shard_map(
        per_device, mesh=mesh, in_specs=in_specs, out_specs=out_specs, check_vma=False
    )
```
